32 devices in a mesh: groups: 2 (over y), tm: 8 (over z, x), height: 2 (over core).
Axes of the slice: x: 2, y: 2, z: 4, core: 2. Of those that a mesh axis runs over, the one named last changes fastest.
Arguments:
- video: bfloat16 [32, 8, 64, 256], P(('groups', 'tm'), 'height'), parts along dimension 0, may hold values from -6 to 6
- block_ids: int32 [32], P('groups'), parts along dimension 0, may hold values from 0 to 4, never falling along the last dimension, each value on 1 to 4 neighbouring positions
- conv_weight: bfloat16 [3, 3, 3, 256, 256], replicated, may hold values from -0.078125 to 0.078125
- w_query: bfloat16 [256, 256], replicated, may hold values from -4 to 4
- w_key: bfloat16 [256, 256], replicated, may hold values from -4 to 4
- w_value: bfloat16 [256, 256], replicated, may hold values from -0.375 to 0.375
- w_output: bfloat16 [256, 256], replicated, may hold values from -0.375 to 0.375
Outputs:
- encoded: bfloat16 [32, 8, 64, 256], P(('groups', 'tm'), 'height'), parts along dimension 0
The draws below stay inside these ranges and needn't reach their ends.
There are 2 independent parts, one for each index of `groups`. The reference program is written for one: setup_inputs(seed, part) draws one part's arguments, and reference() takes and returns one part's arrays. A program takes and returns all parts, laid end to end along the dimension named above; an argument that names none is the same for every part. Nothing has to cross between parts.
Inputs may be any that keep to these rules, and one draw needn't show every extreme that they name: `block_ids`: block ids never fall along the frames and start at 0; each block has 1 to 4 frames, and some block has exactly 4.
All inputs are finite; a program needn't handle non-finite values.
Results may differ from the reference program's by a relative error of at most 0.012.
Values may be sent and summed in bfloat16 or wider, within the bound.
A program may use at most 64 MiB of HBM per device.

```python
import math
import jax
import jax.numpy as jnp
import numpy as np
from jax import lax

C = 256
HD = 64
BLOCK = 4
WIDTH = 64
FRAMES = 16
ROWS = 8
BLOCKS = 5


def pair_weights(key):
    base_key, noise_key = jax.random.split(jax.random.fold_in(key, 11), 2)
    keys_part = jax.random.truncated_normal(base_key, -2.0, 2.0, (C, C), jnp.float32) * C ** (-0.5)
    other = jax.random.truncated_normal(noise_key, -2.0, 2.0, (C, C), jnp.float32) * C ** (-0.5)
    return (keys_part, other)


def draw_w_key(key, part):
    keys_part, other = pair_weights(key)
    return keys_part.astype(jnp.bfloat16)


def draw_w_query(key, part):
    keys_part, other = pair_weights(key)
    return other.astype(jnp.bfloat16)


def shard_levels(own_key, extent, pieces, low, high):
    def one(axis_at, shards_of):
        steps = jax.random.uniform(jax.random.fold_in(jax.random.fold_in(own_key, 6), axis_at), (shards_of,), jnp.float32, low / len(pieces), high / len(pieces))
        return jnp.repeat(jnp.exp(steps), extent[axis_at] // shards_of).reshape((-1,) + (1,) * (len(extent) - axis_at - 1))

    level = one(*pieces[0])
    for cut in pieces[1:]:
        level = level * one(*cut)
    return level


def length_profile(amount, total, bound, slope):
    loads = [(1 << 20) // math.isqrt(grade ** slope) + 1 for grade in range(2, amount + 1)]
    rest, counts = total - bound - (amount - 1), [1] * (amount - 1)
    while rest > 0:
        free = [i for i in range(amount - 1) if counts[i] < bound]
        pool, budget = sum([loads[i] for i in free]), rest
        for i in free:
            addition = min(bound - counts[i], max(1, budget * loads[i] // pool), rest)
            counts[i] = counts[i] + addition
            rest = rest - addition
    return np.array([bound] + counts)


def ragged(stream_key, count, total, bound, lean):
    if count == 2:
        one = jax.random.randint(stream_key, (), max(1, total - bound), min(bound, total - 1) + 1)
        return jnp.stack([one, total - one])
    sizes = jnp.asarray(length_profile(count, total, bound, lean), jnp.int32)
    couples = (count - 1) // 2
    giver, receiver = sizes[1:1 + 2 * couples:2], sizes[2:2 + 2 * couples:2]
    slack = jnp.minimum(giver - 1, bound - receiver)
    moved = jax.random.randint(jax.random.fold_in(stream_key, 1), (couples,), 0, 1 << 20) % (slack + 1)
    sizes = sizes.at[1:1 + 2 * couples:2].set(giver - moved).at[2:2 + 2 * couples:2].set(receiver + moved)
    return sizes[jax.random.permutation(jax.random.fold_in(stream_key, 2), count)]


def gaussian(own_key, dims, spread, most, cuts=(), held_as=jnp.bfloat16):
    loudness = shard_levels(own_key, dims, cuts, -0.22, 0.18) if cuts else 1.0
    entries = jax.random.normal(own_key, dims, jnp.float32) * spread * loudness
    return jnp.minimum(jnp.maximum(entries, -most), most).astype(held_as)


def setup_inputs(seed: int = 0, part: int = 0) -> dict:
    splits = jax.random.split(jax.random.key(seed), 8)
    own_keys = jax.random.split(jax.random.fold_in(splits[7], part), 8)
    video = gaussian(own_keys[0], (FRAMES, ROWS, WIDTH, C), 1.0, 6.0, ((0, 8), (1, 2)))
    block_ids = jnp.searchsorted(jnp.cumsum(ragged(own_keys[1], BLOCKS, FRAMES, BLOCK, 1)), jnp.arange(FRAMES), side="right").astype(jnp.int32)
    conv_weight = gaussian(splits[2], (3, 3, 3, C, C), (27 * C) ** -0.5, 0.078125)
    w_query = draw_w_query(jax.random.fold_in(splits[7], 71), part)
    w_key = draw_w_key(jax.random.fold_in(splits[7], 71), part)
    w_value = gaussian(splits[5], (C, C), C ** -0.5, 0.375)
    w_output = gaussian(splits[6], (C, C), C ** -0.5, 0.375)
    return dict(video=video, block_ids=block_ids, conv_weight=conv_weight, w_query=w_query, w_key=w_key, w_value=w_value, w_output=w_output)


def normalize(values):
    wide = values.astype(jnp.float32)
    return wide * lax.rsqrt(lax.optimization_barrier(jnp.mean(wide * wide, axis=-1, keepdims=True)) + 1e-06)

def project(flat, weight):
    return jnp.dot(flat, weight, preferred_element_type=jnp.float32).astype(jnp.bfloat16)

def reference(video, block_ids, conv_weight, w_query, w_key, w_value, w_output):
    frames, rows, cols, chans = video.shape
    heads = chans // HD
    activated = jax.nn.silu(normalize(video)).astype(jnp.bfloat16)
    padded = jnp.pad(activated, ((2, 0), (1, 1), (1, 1), (0, 0)))
    total = jnp.zeros((frames * rows * cols, chans), jnp.float32)
    for tap_t in range(3):
        for tap_r in range(3):
            for tap_w in range(3):
                window = padded[tap_t:tap_t + frames, tap_r:tap_r + rows, tap_w:tap_w + cols].reshape(-1, chans)
                total = total + jnp.dot(window, conv_weight[tap_t, tap_r, tap_w], preferred_element_type=jnp.float32)
    hidden = (video.astype(jnp.float32) + total.reshape(video.shape)).astype(jnp.bfloat16)
    normed = normalize(hidden).astype(jnp.bfloat16).reshape(-1, chans)
    query = project(normed, w_query).reshape(frames, rows, cols, heads, HD)
    keys = project(normed, w_key).reshape(frames, rows, cols, heads, HD)
    values = project(normed, w_value).reshape(frames, rows, cols, heads, HD)
    order = jnp.arange(frames, dtype=jnp.int32)
    allowed = (order[None, :] <= order[:, None]) & (block_ids[None, :] >= block_ids[:, None] - 1)

    def one_row(packed):
        q_row, k_row, v_row = packed
        scores = jnp.einsum('fwhd,kwhd->whfk', q_row.astype(jnp.float32), k_row.astype(jnp.float32)) * HD ** (-0.5)
        scores = jnp.where(allowed[None, None], scores, -1e+30)
        top = lax.optimization_barrier(jnp.max(scores, axis=-1, keepdims=True))
        expo = jnp.exp(scores - top)
        weights = (expo / lax.optimization_barrier(jnp.sum(expo, axis=-1, keepdims=True))).astype(jnp.bfloat16)
        out = jnp.einsum('whfk,kwhd->fwhd', weights.astype(jnp.float32), v_row.astype(jnp.float32))
        return out.astype(jnp.bfloat16)
    attended = lax.map(one_row, (jnp.moveaxis(query, 1, 0), jnp.moveaxis(keys, 1, 0), jnp.moveaxis(values, 1, 0)))
    attended = jnp.moveaxis(attended, 0, 1).reshape(-1, chans)
    mixed = hidden.astype(jnp.float32).reshape(-1, chans) + jnp.dot(attended, w_output, preferred_element_type=jnp.float32)
    return mixed.astype(jnp.bfloat16).reshape(video.shape)
```

```python
import functools

import jax
import jax.numpy as jnp
from jax import lax
from jax.experimental import pallas as pl
from jax.experimental.pallas import tpu as pltpu
from jax.sharding import PartitionSpec as P

HD = 64
REACH = 7
MESH = pl.DeviceIdType.MESH


def normalize(wide):
    return wide * lax.rsqrt(jnp.mean(wide * wide, axis=-1, keepdims=True) + 1e-06)


def kernel(n, ids, video, conv_w, w_q, w_k, w_v, w_o, out,
           raw, act, cw, pw, acc, hid, nb, qs, ks, vs, sc, enc, gather, spread,
           load_sem, weight_sem, x_send, x_recv, z_send, z_recv, c_send, e_send, e_recv,
           nb_send, nb_recv, own_out, out_send, out_recv):
    count, rows, cols, chans = video.shape
    half = rows // 2
    own = 2 * count
    heads = chans // HD
    lanes = (REACH + 1) * own * heads
    bf = jnp.bfloat16
    me = lax.axis_index("tm")
    core = lax.axis_index("height")
    side = lax.rem(me, 2)
    even = side == 0
    odd = side == 1
    flip = side + core - 2 * side * core
    partner = {"tm": me + 1 - 2 * side}
    other = {"height": 1 - core}
    below = {"tm": me + 2}
    has_up = me >= 2
    has_far = me >= 4
    has_down = me <= n - 3
    mine = 2 + 2 * side
    theirs = 4 - 2 * side

    def row_of(line, flipped):
        return line - 1 + flipped * (rows - 1 - 2 * (line - 1))

    loads = {}
    for i in (1, 2, 3):
        loads[i] = pltpu.make_async_copy(
            video.at[:, row_of(i, flip)], raw.at[pl.ds(mine, 2), i], load_sem.at[i])
        loads[i].start()

    def weight_load(a):
        return pltpu.make_async_copy(conv_w.at[a], cw.at[a], weight_sem.at[a])

    first_tap = 2 * side
    last_tap = 2 - 2 * side
    for a in (first_tap, 1, last_tap):
        weight_load(a).start()
    p_loads = []
    for j, w in enumerate((w_q, w_k, w_v, w_o)):
        p_loads.append(pltpu.make_async_copy(
            w, pw.at[:, j * chans:(j + 1) * chans], weight_sem.at[3 + j]))
        p_loads[-1].start()

    barrier = pltpu.get_barrier_semaphore()
    pl.semaphore_signal(barrier, inc=1, device_id=partner, device_id_type=MESH)
    pl.semaphore_signal(barrier, inc=1, device_id=other, device_id_type=MESH)

    @pl.when(has_up)
    def _():
        pl.semaphore_signal(barrier, inc=1, device_id={"tm": me - 2}, device_id_type=MESH)

    @pl.when(has_down)
    def _():
        pl.semaphore_signal(barrier, inc=1, device_id=below, device_id_type=MESH)

    @pl.when(even)
    def _():
        for e in range(6):
            act[e, 0] = jnp.zeros((cols, 3 * chans), bf)

    @pl.when(jnp.logical_not(has_up))
    def _():
        for e in range(2):
            for i in range(4):
                act[e, i] = jnp.zeros((cols, 3 * chans), bf)
        for r in range(half):
            for s in range(own - 1, REACH):
                nb[r, s] = jnp.zeros((cols, chans), bf)

    @pl.when(jnp.logical_not(has_far))
    def _():
        for r in range(half):
            for s in range(own - 1):
                nb[r, s] = jnp.zeros((cols, chans), bf)

    ch = lax.broadcasted_iota(jnp.int32, (chans, lanes), 0) // HD
    ln = lax.rem(lax.broadcasted_iota(jnp.int32, (chans, lanes), 1), heads)
    gather[...] = jnp.where(ch == ln, HD ** (-0.5), 0.0).astype(bf)
    ch = lax.broadcasted_iota(jnp.int32, (lanes, chans), 1) // HD
    ln = lax.rem(lax.broadcasted_iota(jnp.int32, (lanes, chans), 0), heads)
    spread[...] = jnp.where(ch == ln, 1.0, 0.0).astype(bf)

    inside = has_up & has_down

    @pl.when(inside)
    def _():
        pl.semaphore_wait(barrier, 4)

    @pl.when(jnp.logical_not(inside))
    def _():
        pl.semaphore_wait(barrier, 3)

    def remote(src, dst, send_sem, recv_sem, device):
        return pltpu.make_async_remote_copy(
            src_ref=src, dst_ref=dst, send_sem=send_sem, recv_sem=recv_sem,
            device_id=device, device_id_type=MESH)

    def x_copy(i):
        return remote(video.at[:, row_of(i, 1 - flip)], raw.at[pl.ds(mine, 2), i],
                      x_send.at[i], x_recv.at[i], partner)

    def x_wait(i):
        at = raw.at[pl.ds(theirs, 2), i]
        remote(at, at, x_send.at[i], x_recv.at[i], partner).wait_recv()

    def z_copy(i):
        return remote(video.at[:, row_of(i, flip)], raw.at[0:2, i], z_send.at[i], z_recv.at[i], below)

    def z_forward(i):
        return remote(raw.at[4:6, i], raw.at[0:2, i], z_send.at[i], z_recv.at[i], below)

    def z_wait(i):
        z_forward(i).wait_recv()

    def c_copy():
        return remote(raw.at[0:2, 2], raw.at[0:2, 3], c_send, z_recv.at[3], partner)

    def e_copy(j):
        src = (raw.at[0:2, 1], raw.at[2:4, 1], video.at[:, row_of(1, flip)])[j]
        return remote(src, raw.at[2 * j:2 * j + 2, 0], e_send.at[j], e_recv.at[j], other)

    x_copy(1).start()
    x_copy(2).start()
    x_copy(3).start()

    @pl.when(odd)
    def _():
        e_copy(2).start()

    @pl.when(odd & has_down)
    def _():
        for i in (1, 2, 3):
            z_copy(i).start()

    col = lax.broadcasted_iota(jnp.int32, (cols, chans), 0)

    def activate(e, i):
        v = normalize(raw[e, i].astype(jnp.float32))
        v = v / (1.0 + jnp.exp(-v))
        act[e, i, :, chans:2 * chans] = v.astype(bf)
        left = jnp.where(col == 0, 0.0, pltpu.roll(v, 1, 0))
        right = jnp.where(col == cols - 1, 0.0, pltpu.roll(v, cols - 1, 0))
        act[e, i, :, 0:chans] = left.astype(bf)
        act[e, i, :, 2 * chans:3 * chans] = right.astype(bf)

    def activate_two(e, i):
        activate(e, i)
        activate(e + 1, i)

    def taps(e, line, size, a):
        total = None
        for o in range(3):
            window = act[pl.ds(e, 2), line + o - 1:line + o - 1 + size]
            term = jnp.dot(window.reshape(2 * size * cols, 3 * chans), cw[a, o + flip * (2 - 2 * o)],
                           preferred_element_type=jnp.float32)
            total = term if total is None else total + term
        return total

    for i in (1, 2, 3):
        loads[i].wait()
        activate_two(mine, i)

    @pl.when(odd)
    def _():
        e_copy(2).wait_recv()
        activate_two(4, 0)

    weight_load(first_tap).wait()
    acc[1] = taps(mine, 1, 2, first_tap).reshape(2, half, cols, chans)

    def nb_copy(m, r):
        src, dst = ((slice(REACH + 2, REACH + 4), slice(5, 7)),
                    (slice(REACH, REACH + 2), slice(3, 5)),
                    (slice(4, 7), slice(0, 3)))[m]
        return remote(nb.at[r, src], nb.at[r, dst], nb_send.at[m, r], nb_recv.at[m, r], below)

    def finish(pair, r, total):
        mixed = raw[2 + 2 * pair:4 + 2 * pair, 1 + r].astype(jnp.float32) + total.reshape(2, cols, chans)
        hidden = mixed.astype(bf)
        hid[r, 2 * pair:2 * pair + 2] = hidden
        nb[r, REACH + 2 * pair:REACH + 2 * pair + 2] = normalize(hidden.astype(jnp.float32)).astype(bf)

        @pl.when(has_down)
        def _():
            nb_copy(1 - pair, r).start()

    def late(r):
        total = acc[1, :, r].reshape(2 * cols, chans)
        total = total + taps(theirs, 1 + r, 1, last_tap) + taps(3, 1 + r, 1, 1)
        finish(1, r, total)

    def early(r):
        total = acc[0, :, r].reshape(2 * cols, chans)
        total = total + taps(1, 1 + r, 1, 1) + taps(0, 1 + r, 1, 0)
        finish(0, r, total)

    for i in (1, 2):
        x_wait(i)

        @pl.when(even & has_down)
        def _(i=i):
            z_forward(i).start()

        if i == 1:
            @pl.when(odd)
            def _():
                e_copy(1).start()
        activate_two(theirs, i)

    @pl.when(odd)
    def _():
        e_copy(1).wait_recv()
        activate_two(2, 0)

    weight_load(1).wait()
    weight_load(last_tap).wait()
    late(0)
    x_wait(3)
    activate_two(theirs, 3)
    late(1)

    @pl.when(odd & has_up)
    def _():
        z_wait(1)
        e_copy(0).start()
        z_wait(2)
        c_copy().start()

    acc[0] = taps(2, 1, 2, 2).reshape(2, half, cols, chans)

    @pl.when(odd & has_up)
    def _():
        activate_two(0, 1)
        activate_two(0, 2)
        e_copy(0).wait_recv()
        activate_two(0, 0)

    @pl.when(even & has_up)
    def _():
        z_wait(1)
        activate_two(0, 1)
        z_wait(2)
        activate_two(0, 2)

    early(0)

    @pl.when(has_up)
    def _():
        z_wait(3)
        activate_two(0, 3)

    early(1)

    for load in p_loads:
        load.wait()

    def keyed(r, start, size):
        x = nb[r, start:start + size].reshape(size * cols, chans)
        got = jnp.dot(x, pw[:, chans:3 * chans], preferred_element_type=jnp.float32).astype(bf)
        ks[r, start:start + size] = got[:, :chans].reshape(size, cols, chans)
        vs[r, start:start + size] = got[:, chans:].reshape(size, cols, chans)

    def asked(r):
        x = nb[r, REACH:REACH + own].reshape(own * cols, chans)
        got = jnp.dot(x, pw[:, :chans], preferred_element_type=jnp.float32).astype(bf)
        qs[r] = got.reshape(own, cols, chans)

    frames = ids.shape[0]
    lane = lax.broadcasted_iota(jnp.int32, (1, lanes), 1)
    spot = lane // heads
    key_at = lane // (heads * own)
    which = lax.rem(spot, own)
    first = 2 * (me - side)
    key_id = jnp.zeros((1, lanes), jnp.int32)
    for s in range(REACH + own):
        key_id = jnp.where(key_at + which == s, ids[lax.rem(first - REACH + s + frames, frames)], key_id)
    query_id = jnp.zeros((1, lanes), jnp.int32)
    for f in range(own):
        query_id = jnp.where(which == f, ids[first + f], query_id)
    allowed = (first - REACH + key_at + which >= 0) & (key_id >= query_id - 1)
    spots = lax.broadcasted_iota(jnp.int32, (cols, lanes), 1) // heads

    def scored(r, scores, f, keys):
        prods = [qs[r, f] * ks[r, f + j] for j in keys]
        got = jnp.dot(jnp.concatenate(prods, axis=0), gather[...], preferred_element_type=jnp.float32)
        for at, j in enumerate(keys):
            scores = jnp.where(spots == j * own + f, got[at * cols:(at + 1) * cols], scores)
        return scores

    def near_scores(r):
        scores = jnp.zeros((cols, lanes), jnp.float32)
        for f in range(own):
            scores = scored(r, scores, f, range(own - 1 - f, REACH + 1))
        sc[r] = scores

    def out_copy(r):
        at = out.at[:, row_of(1 + r, flip)]
        keep = pltpu.make_async_copy(enc.at[r, pl.ds(2 * side, 2)], at, own_out.at[r])
        give = remote(enc.at[r, pl.ds(2 - 2 * side, 2)], at, out_send.at[r], out_recv.at[r], partner)
        return keep, give

    def out_wait(r):
        at = out.at[:, row_of(1 + r, 1 - flip)]
        remote(enc.at[r, pl.ds(2 - 2 * side, 2)], at, out_send.at[r], out_recv.at[r], partner).wait_recv()

    def attend(r):
        scores = sc[r]
        for f in range(own - 1):
            scores = scored(r, scores, f, range(own - 1 - f))
        scores = jnp.where(allowed, scores, -1e30)
        steps = [heads * own * 2 ** i for i in range((REACH + 1).bit_length() - 1)]
        top = scores
        for by in steps:
            top = jnp.maximum(top, pltpu.roll(top, by, 1))
        expo = jnp.exp(scores - top)
        total = expo
        for by in steps:
            total = total + pltpu.roll(total, by, 1)
        weights = expo / total
        parts = []
        for f in range(own):
            picked = [jnp.where(spots == j * own + f, weights, 0.0).astype(bf) for j in range(REACH + 1)]
            wide = jnp.dot(jnp.concatenate(picked, axis=0), spread[...], preferred_element_type=jnp.float32)
            got = jnp.zeros((cols, chans), jnp.float32)
            for j in range(REACH + 1):
                got = got + wide[j * cols:(j + 1) * cols] * vs[r, f + j].astype(jnp.float32)
            parts.append(got.astype(bf))
        mixed = jnp.dot(jnp.concatenate(parts, axis=0), pw[:, 3 * chans:], preferred_element_type=jnp.float32)
        mixed = mixed + hid[r].astype(jnp.float32).reshape(own * cols, chans)
        enc[r] = mixed.astype(bf).reshape(own, cols, chans)
        for copy in out_copy(r):
            copy.start()

    def take(m, r):
        @pl.when(has_up if m < 2 else has_far)
        def _():
            nb_copy(m, r).wait_recv()

    for r in range(half):
        asked(r)
        keyed(r, REACH, own)
    for r in range(half):
        take(0, r)
        take(1, r)

        @pl.when(inside)
        def _(r=r):
            nb_copy(2, r).start()

    for r in range(half):
        keyed(r, 3, 4)
        near_scores(r)
    for r in range(half):
        take(2, r)
        keyed(r, 0, 3)
        attend(r)

    for i in (1, 2, 3):
        x_copy(i).wait_send()

    @pl.when(has_down)
    def _():
        z_forward(1).wait_send()
        z_forward(2).wait_send()
        for r in range(half):
            nb_copy(0, r).wait_send()
            nb_copy(1, r).wait_send()

    @pl.when(odd & has_down)
    def _():
        z_forward(3).wait_send()

    @pl.when(inside)
    def _():
        for r in range(half):
            nb_copy(2, r).wait_send()

    @pl.when(odd)
    def _():
        e_copy(1).wait_send()
        e_copy(2).wait_send()

    @pl.when(odd & has_up)
    def _():
        e_copy(0).wait_send()
        c_copy().wait_send()

    for r in range(half):
        keep, give = out_copy(r)
        keep.wait()
        give.wait_send()
        out_wait(r)


def per_device(video, block_ids, conv_weight, w_query, w_key, w_value, w_output):
    count, rows, cols, chans = video.shape
    n = lax.axis_size("tm")
    assert count == 2 and n % 2 == 0 and n >= 4 and lax.axis_size("height") == 2
    assert rows == 4
    half = rows // 2
    own = 2 * count
    lanes = (REACH + 1) * own * (chans // HD)
    seen = REACH + own
    bf = jnp.bfloat16
    dma = pltpu.SemaphoreType.DMA
    anywhere = pl.BlockSpec(memory_space=pl.ANY)
    return pl.pallas_call(
        functools.partial(kernel, n),
        out_shape=jax.ShapeDtypeStruct(video.shape, bf),
        in_specs=[pl.BlockSpec(memory_space=pltpu.SMEM)] + [anywhere] * 6,
        out_specs=anywhere,
        scratch_shapes=[
            pltpu.VMEM((6, 4, cols, chans), bf),
            pltpu.VMEM((6, 4, cols, 3 * chans), bf),
            pltpu.VMEM((3, 3, 3 * chans, chans), bf),
            pltpu.VMEM((chans, 4 * chans), bf),
            pltpu.VMEM((2, 2, half, cols, chans), jnp.float32),
            pltpu.VMEM((half, own, cols, chans), bf),
            pltpu.VMEM((half, seen, cols, chans), bf),
            pltpu.VMEM((half, own, cols, chans), bf),
            pltpu.VMEM((half, seen, cols, chans), bf),
            pltpu.VMEM((half, seen, cols, chans), bf),
            pltpu.VMEM((half, cols, lanes), jnp.float32),
            pltpu.VMEM((half, own, cols, chans), bf),
            pltpu.VMEM((chans, lanes), bf),
            pltpu.VMEM((lanes, chans), bf),
            dma((4,)),
            dma((7,)),
            dma((4,)),
            dma((4,)),
            dma((4,)),
            dma((4,)),
            dma,
            dma((3,)),
            dma((3,)),
            dma((3, half)),
            dma((3, half)),
            dma((half,)),
            dma((half,)),
            dma((half,)),
        ],
        compiler_params=pltpu.CompilerParams(
            collective_id=0, has_side_effects=True, vmem_limit_bytes=63 * 1024 * 1024),
    )(block_ids, video, conv_weight.reshape(3, 3, 3 * chans, chans), w_query, w_key, w_value, w_output)


def solution(mesh):
    placed = (P(("groups", "tm"), "height", None, None), P("groups"), P(), P(), P(), P(), P())
    return jax.shard_map(
        per_device,
        mesh=mesh,
        in_specs=placed,
        out_specs=P(("groups", "tm"), "height", None, None),
        check_vma=False,
    )
```

```python
import functools

import jax
import jax.numpy as jnp
from jax import lax
from jax.experimental import pallas as pl
from jax.experimental.pallas import tpu as pltpu
from jax.sharding import PartitionSpec as P

HD = 64
REACH = 7
MESH = pl.DeviceIdType.MESH


def normalize(wide):
    return wide * lax.rsqrt(jnp.mean(wide * wide, axis=-1, keepdims=True) + 1e-06)


def kernel(n, ids, video, conv_w, w_q, w_k, w_v, w_o, out,
           raw, act, cw, pw, acc, hid, nb, qs, ks, vs, tops, totals, gots, enc, gather,
           load_sem, weight_sem, x_send, x_recv, z_send, z_recv, c_send, e_send, e_recv,
           nb_send, nb_recv, own_out, out_send, out_recv):
    count, rows, cols, chans = video.shape
    half = rows // 2
    own = 2 * count
    bf = jnp.bfloat16
    me = lax.axis_index("tm")
    core = lax.axis_index("height")
    side = lax.rem(me, 2)
    even = side == 0
    odd = side == 1
    flip = side + core - 2 * side * core
    partner = {"tm": me + 1 - 2 * side}
    other = {"height": 1 - core}
    below = {"tm": me + 2}
    has_up = me >= 2
    has_far = me >= 4
    has_down = me <= n - 3
    mine = 2 + 2 * side
    theirs = 4 - 2 * side

    def row_of(line, flipped):
        return line - 1 + flipped * (rows - 1 - 2 * (line - 1))

    barrier = pltpu.get_barrier_semaphore()
    pl.semaphore_signal(barrier, inc=1, device_id=partner, device_id_type=MESH)
    pl.semaphore_signal(barrier, inc=1, device_id=other, device_id_type=MESH)

    @pl.when(has_up)
    def _():
        pl.semaphore_signal(barrier, inc=1, device_id={"tm": me - 2}, device_id_type=MESH)

    @pl.when(has_down)
    def _():
        pl.semaphore_signal(barrier, inc=1, device_id=below, device_id_type=MESH)

    loads = {}
    for i in (1, 2, 3):
        loads[i] = pltpu.make_async_copy(
            video.at[:, row_of(i, flip)], raw.at[pl.ds(mine, 2), i], load_sem.at[i])
        loads[i].start()

    def weight_load(a):
        return pltpu.make_async_copy(conv_w.at[a], cw.at[a], weight_sem.at[a])

    first_tap = 2 * side
    last_tap = 2 - 2 * side
    for a in (first_tap, 1, last_tap):
        weight_load(a).start()
    p_loads = []
    for j, w in enumerate((w_q, w_k, w_v, w_o)):
        p_loads.append(pltpu.make_async_copy(
            w, pw.at[:, j * chans:(j + 1) * chans], weight_sem.at[3 + j]))
        p_loads[-1].start()

    inside = has_up & has_down

    @pl.when(inside)
    def _():
        pl.semaphore_wait(barrier, 4)

    @pl.when(jnp.logical_not(inside))
    def _():
        pl.semaphore_wait(barrier, 3)

    def remote(src, dst, send_sem, recv_sem, device):
        return pltpu.make_async_remote_copy(
            src_ref=src, dst_ref=dst, send_sem=send_sem, recv_sem=recv_sem,
            device_id=device, device_id_type=MESH)

    def x_copy(i):
        return remote(video.at[:, row_of(i, 1 - flip)], raw.at[pl.ds(mine, 2), i],
                      x_send.at[i], x_recv.at[i], partner)

    def x_wait(i):
        at = raw.at[pl.ds(theirs, 2), i]
        remote(at, at, x_send.at[i], x_recv.at[i], partner).wait_recv()

    def z_copy(i):
        return remote(video.at[:, row_of(i, flip)], raw.at[0:2, i], z_send.at[i], z_recv.at[i], below)

    def z_forward(i):
        return remote(raw.at[4:6, i], raw.at[0:2, i], z_send.at[i], z_recv.at[i], below)

    def z_wait(i):
        z_forward(i).wait_recv()

    def c_copy():
        return remote(raw.at[0:2, 2], raw.at[0:2, 3], c_send, z_recv.at[3], partner)

    def e_copy(j):
        src = (raw.at[0:2, 1], raw.at[2:4, 1], video.at[:, row_of(1, flip)])[j]
        return remote(src, raw.at[2 * j:2 * j + 2, 0], e_send.at[j], e_recv.at[j], other)

    x_copy(1).start()
    x_copy(2).start()
    x_copy(3).start()

    @pl.when(odd)
    def _():
        e_copy(2).start()

    @pl.when(odd & has_down)
    def _():
        for i in (1, 2, 3):
            z_copy(i).start()

    @pl.when(even)
    def _():
        for e in range(6):
            act[e, 0] = jnp.zeros((cols, 3 * chans), bf)

    @pl.when(jnp.logical_not(has_up))
    def _():
        for e in range(2):
            for i in range(4):
                act[e, i] = jnp.zeros((cols, 3 * chans), bf)
        for r in range(half):
            for s in range(own - 1, REACH):
                nb[r, s] = jnp.zeros((cols, chans), bf)

    @pl.when(jnp.logical_not(has_far))
    def _():
        for r in range(half):
            for s in range(own - 1):
                nb[r, s] = jnp.zeros((cols, chans), bf)

    head_of = [lax.broadcasted_iota(jnp.int32, (chans, chans), d) // HD for d in range(2)]
    gather[...] = jnp.where(head_of[0] == head_of[1], HD ** (-0.5), 0.0).astype(bf)

    col = lax.broadcasted_iota(jnp.int32, (cols, chans), 0)

    def activate(e, i):
        v = normalize(raw[e, i].astype(jnp.float32))
        v = v / (1.0 + jnp.exp(-v))
        act[e, i, :, chans:2 * chans] = v.astype(bf)
        left = jnp.where(col == 0, 0.0, pltpu.roll(v, 1, 0))
        right = jnp.where(col == cols - 1, 0.0, pltpu.roll(v, cols - 1, 0))
        act[e, i, :, 0:chans] = left.astype(bf)
        act[e, i, :, 2 * chans:3 * chans] = right.astype(bf)

    def activate_two(e, i):
        activate(e, i)
        activate(e + 1, i)

    def taps(e, line, size, a):
        total = None
        for o in range(3):
            window = act[pl.ds(e, 2), line + o - 1:line + o - 1 + size]
            term = jnp.dot(window.reshape(2 * size * cols, 3 * chans), cw[a, o + flip * (2 - 2 * o)],
                           preferred_element_type=jnp.float32)
            total = term if total is None else total + term
        return total

    for i in (1, 2, 3):
        loads[i].wait()
        activate_two(mine, i)

    @pl.when(odd)
    def _():
        e_copy(2).wait_recv()
        activate_two(4, 0)

    weight_load(first_tap).wait()
    acc[1] = taps(mine, 1, 2, first_tap).reshape(2, half, cols, chans)

    def nb_copy(m, r):
        src, dst = ((slice(REACH + 2, REACH + 4), slice(5, 7)),
                    (slice(REACH, REACH + 2), slice(3, 5)),
                    (slice(6, 7), slice(2, 3)),
                    (slice(5, 6), slice(1, 2)),
                    (slice(4, 5), slice(0, 1)))[m]
        return remote(nb.at[r, src], nb.at[r, dst], nb_send.at[m, r], nb_recv.at[m, r], below)

    def finish(pair, r, total):
        mixed = raw[2 + 2 * pair:4 + 2 * pair, 1 + r].astype(jnp.float32) + total.reshape(2, cols, chans)
        hidden = mixed.astype(bf)
        hid[r, 2 * pair:2 * pair + 2] = hidden
        nb[r, REACH + 2 * pair:REACH + 2 * pair + 2] = normalize(hidden.astype(jnp.float32)).astype(bf)

        @pl.when(has_down)
        def _():
            nb_copy(1 - pair, r).start()

    def late(r):
        total = acc[1, :, r].reshape(2 * cols, chans)
        total = total + taps(theirs, 1 + r, 1, last_tap) + taps(3, 1 + r, 1, 1)
        finish(1, r, total)

    def early(r):
        total = acc[0, :, r].reshape(2 * cols, chans)
        total = total + taps(1, 1 + r, 1, 1) + taps(0, 1 + r, 1, 0)
        finish(0, r, total)

    for i in (1, 2):
        x_wait(i)

        @pl.when(even & has_down)
        def _(i=i):
            z_forward(i).start()

        if i == 1:
            @pl.when(odd)
            def _():
                e_copy(1).start()
        activate_two(theirs, i)

    @pl.when(odd)
    def _():
        e_copy(1).wait_recv()
        activate_two(2, 0)

    @pl.when(odd & has_up)
    def _():
        z_wait(1)
        e_copy(0).start()

    weight_load(1).wait()
    weight_load(last_tap).wait()
    late(0)
    x_wait(3)

    @pl.when(odd & has_up)
    def _():
        z_wait(2)
        c_copy().start()

    activate_two(theirs, 3)
    late(1)

    acc[0] = taps(2, 1, 2, 2).reshape(2, half, cols, chans)

    @pl.when(odd & has_up)
    def _():
        activate_two(0, 1)
        activate_two(0, 2)
        e_copy(0).wait_recv()
        activate_two(0, 0)

    @pl.when(even & has_up)
    def _():
        z_wait(1)
        activate_two(0, 1)
        z_wait(2)
        activate_two(0, 2)

    early(0)

    @pl.when(has_up)
    def _():
        z_wait(3)
        activate_two(0, 3)

    early(1)

    for load in p_loads:
        load.wait()

    def keyed(r, start, size):
        x = nb[r, start:start + size].reshape(size * cols, chans)
        got = jnp.dot(x, pw[:, chans:3 * chans], preferred_element_type=jnp.float32).astype(bf)
        ks[r, start:start + size] = got[:, :chans].reshape(size, cols, chans)
        vs[r, start:start + size] = got[:, chans:].reshape(size, cols, chans)

    def asked(r):
        x = nb[r, REACH:REACH + own].reshape(own * cols, chans)
        got = jnp.dot(x, pw[:, :chans], preferred_element_type=jnp.float32).astype(bf)
        qs[r] = got.reshape(own, cols, chans)

    frames = ids.shape[0]
    first = 2 * (me - side)
    key_ids = [ids[lax.rem(first - REACH + s + frames, frames)] for s in range(REACH + own)]
    bias = {}
    for f in range(own):
        for s in range(f, f + REACH + 1):
            allowed = (first - REACH + s >= 0) & (key_ids[s] >= key_ids[REACH + f] - 1)
            bias[f, s] = jnp.where(allowed, 0.0, -1e30)

    def scored(r, pairs):
        prods = [qs[r, f] * ks[r, s] for f, s in pairs]
        got = jnp.dot(jnp.concatenate(prods, axis=0), gather[...], preferred_element_type=jnp.float32)
        return [got[at * cols:(at + 1) * cols] + bias[pair] for at, pair in enumerate(pairs)]

    def out_copy(r, f):
        at = out.at[f % 2, row_of(1 + r, flip)]
        keep = pltpu.make_async_copy(enc.at[r, f], at, own_out.at[r, f % 2])
        give = remote(enc.at[r, f], at, out_send.at[r, f % 2], out_recv.at[r, f % 2], partner)
        return keep, give

    def out_wait(r, f):
        at = out.at[f, row_of(1 + r, 1 - flip)]
        remote(enc.at[r, f], at, out_send.at[r, f], out_recv.at[r, f], partner).wait_recv()

    def settle(r, f, total, got):
        mixed = jnp.dot((got / total).astype(bf), pw[:, 3 * chans:], preferred_element_type=jnp.float32)
        enc[r, f] = (mixed + hid[r, f].astype(jnp.float32)).astype(bf)
        keep, give = out_copy(r, f)

        @pl.when(side == f // 2)
        def _():
            keep.start()

        @pl.when(side != f // 2)
        def _():
            give.start()

    def near(r, f):
        keys = range(own - 1, f + REACH + 1)
        scores = scored(r, [(f, s) for s in keys])
        top = functools.reduce(jnp.maximum, scores)
        total = got = None
        for s, score in zip(keys, scores):
            weight = jnp.exp(score - top)
            term = weight * vs[r, s].astype(jnp.float32)
            total = weight if total is None else total + weight
            got = term if got is None else got + term
        if f == own - 1:
            settle(r, f, total, got)
        else:
            tops[r, f], totals[r, f], gots[r, f] = top, total, got

    def far(r, s):
        queries = range(s, -1, -1)
        for f, score in zip(queries, scored(r, [(f, s) for f in queries])):
            top = jnp.maximum(tops[r, f], score)
            shrink = jnp.exp(tops[r, f] - top)
            weight = jnp.exp(score - top)
            total = totals[r, f] * shrink + weight
            got = gots[r, f] * shrink + weight * vs[r, s].astype(jnp.float32)
            if f == s:
                settle(r, f, total, got)
            else:
                tops[r, f], totals[r, f], gots[r, f] = top, total, got

    def take(m, r):
        @pl.when(has_up if m < 2 else has_far)
        def _():
            nb_copy(m, r).wait_recv()

    def relay(r, which_ones):
        @pl.when(inside)
        def _():
            for m in which_ones:
                nb_copy(m, r).start()

    for r in range(half):
        asked(r)
        keyed(r, REACH, own)
    take(0, 0)
    relay(0, (2, 3))
    keyed(0, 5, 2)
    take(1, 0)
    relay(0, (4,))
    take(0, 1)
    relay(1, (2, 3))
    keyed(0, 3, 2)
    keyed(1, 5, 2)
    for f in range(own - 1, -1, -1):
        near(0, f)
    take(1, 1)
    relay(1, (4,))
    keyed(1, 3, 2)
    for f in range(own - 1, -1, -1):
        near(1, f)
    for r in range(half):
        for s in range(own - 2, -1, -1):
            take(4 - s, r)
            keyed(r, s, 1)
            far(r, s)

    for i in (1, 2, 3):
        x_copy(i).wait_send()

    @pl.when(has_down)
    def _():
        z_forward(1).wait_send()
        z_forward(2).wait_send()
        for r in range(half):
            nb_copy(0, r).wait_send()
            nb_copy(1, r).wait_send()

    @pl.when(odd & has_down)
    def _():
        z_forward(3).wait_send()

    @pl.when(inside)
    def _():
        for r in range(half):
            for m in (2, 3, 4):
                nb_copy(m, r).wait_send()

    @pl.when(odd)
    def _():
        e_copy(1).wait_send()
        e_copy(2).wait_send()

    @pl.when(odd & has_up)
    def _():
        e_copy(0).wait_send()
        c_copy().wait_send()

    for r in range(half):
        for f in range(2):
            keep, give = out_copy(r, f)
            keep.wait()
            give.wait_send()
            out_wait(r, f)


def per_device(video, block_ids, conv_weight, w_query, w_key, w_value, w_output):
    count, rows, cols, chans = video.shape
    n = lax.axis_size("tm")
    assert count == 2 and n % 2 == 0 and n >= 4 and lax.axis_size("height") == 2
    assert rows == 4
    half = rows // 2
    own = 2 * count
    seen = REACH + own
    bf = jnp.bfloat16
    dma = pltpu.SemaphoreType.DMA
    anywhere = pl.BlockSpec(memory_space=pl.ANY)
    operands = [pltpu.with_memory_space_constraint(v, pltpu.HBM) for v in (
        block_ids, video, conv_weight.reshape(3, 3, 3 * chans, chans), w_query, w_key, w_value, w_output)]
    return pl.pallas_call(
        functools.partial(kernel, n),
        out_shape=jax.ShapeDtypeStruct(video.shape, bf),
        in_specs=[pl.BlockSpec(memory_space=pltpu.SMEM)] + [anywhere] * 6,
        out_specs=anywhere,
        scratch_shapes=[
            pltpu.VMEM((6, 4, cols, chans), bf),
            pltpu.VMEM((6, 4, cols, 3 * chans), bf),
            pltpu.VMEM((3, 3, 3 * chans, chans), bf),
            pltpu.VMEM((chans, 4 * chans), bf),
            pltpu.VMEM((2, 2, half, cols, chans), jnp.float32),
            pltpu.VMEM((half, own, cols, chans), bf),
            pltpu.VMEM((half, seen, cols, chans), bf),
            pltpu.VMEM((half, own, cols, chans), bf),
            pltpu.VMEM((half, seen, cols, chans), bf),
            pltpu.VMEM((half, seen, cols, chans), bf),
            pltpu.VMEM((half, own - 1, cols, chans), jnp.float32),
            pltpu.VMEM((half, own - 1, cols, chans), jnp.float32),
            pltpu.VMEM((half, own - 1, cols, chans), jnp.float32),
            pltpu.VMEM((half, own, cols, chans), bf),
            pltpu.VMEM((chans, chans), bf),
            dma((4,)),
            dma((7,)),
            dma((4,)),
            dma((4,)),
            dma((4,)),
            dma((4,)),
            dma,
            dma((3,)),
            dma((3,)),
            dma((5, half)),
            dma((5, half)),
            dma((half, 2)),
            dma((half, 2)),
            dma((half, 2)),
        ],
        compiler_params=pltpu.CompilerParams(
            collective_id=0, has_side_effects=True, vmem_limit_bytes=40 * 1024 * 1024),
    )(*operands)


def solution(mesh):
    placed = (P(("groups", "tm"), "height", None, None), P("groups"), P(), P(), P(), P(), P())
    return jax.shard_map(
        per_device,
        mesh=mesh,
        in_specs=placed,
        out_specs=P(("groups", "tm"), "height", None, None),
        check_vma=False,
    )
```

```python
import functools

import jax
import jax.numpy as jnp
from jax import lax
from jax.experimental import pallas as pl
from jax.experimental.pallas import tpu as pltpu
from jax.sharding import PartitionSpec as P

HD = 64
REACH = 7
MESH = pl.DeviceIdType.MESH


def normalize(wide):
    return wide * lax.rsqrt(jnp.mean(wide * wide, axis=-1, keepdims=True) + 1e-06)


def kernel(n, ids, video, conv_w, w_q, w_k, w_v, w_o, out,
           raw, act, cw, pw, acc, hid, nb, qs, ks, vs, tops, totals, gots, enc, gather,
           load_sem, weight_sem, x_send, x_recv, z_send, z_recv, c_send, e_send, e_recv,
           nb_send, nb_recv, own_out, out_send, out_recv):
    count, rows, cols, chans = video.shape
    half = rows // 2
    own = 2 * count
    bf = jnp.bfloat16
    me = lax.axis_index("tm")
    core = lax.axis_index("height")
    side = lax.rem(me, 2)
    even = side == 0
    odd = side == 1
    flip = side + core - 2 * side * core
    partner = {"tm": me + 1 - 2 * side}
    other = {"height": 1 - core}
    below = {"tm": me + 2}
    has_up = me >= 2
    has_far = me >= 4
    has_down = me <= n - 3
    mine = 2 + 2 * side
    theirs = 4 - 2 * side

    def row_of(line, flipped):
        return line - 1 + flipped * (rows - 1 - 2 * (line - 1))

    barrier = pltpu.get_barrier_semaphore()
    pl.semaphore_signal(barrier, inc=1, device_id=partner, device_id_type=MESH)
    pl.semaphore_signal(barrier, inc=1, device_id=other, device_id_type=MESH)

    @pl.when(has_up)
    def _():
        pl.semaphore_signal(barrier, inc=1, device_id={"tm": me - 2}, device_id_type=MESH)

    @pl.when(has_down)
    def _():
        pl.semaphore_signal(barrier, inc=1, device_id=below, device_id_type=MESH)

    loads = {}
    for i in (1, 2, 3):
        loads[i] = pltpu.make_async_copy(
            video.at[:, row_of(i, flip)], raw.at[pl.ds(mine, 2), i], load_sem.at[i])
        loads[i].start()

    def weight_load(a):
        return pltpu.make_async_copy(conv_w.at[a], cw.at[a], weight_sem.at[a])

    first_tap = 2 * side
    last_tap = 2 - 2 * side
    for a in (first_tap, 1, last_tap):
        weight_load(a).start()
    p_loads = []
    for j, w in enumerate((w_q, w_k, w_v, w_o)):
        p_loads.append(pltpu.make_async_copy(
            w, pw.at[:, j * chans:(j + 1) * chans], weight_sem.at[3 + j]))
        p_loads[-1].start()

    inside = has_up & has_down

    @pl.when(inside)
    def _():
        pl.semaphore_wait(barrier, 4)

    @pl.when(jnp.logical_not(inside))
    def _():
        pl.semaphore_wait(barrier, 3)

    def remote(src, dst, send_sem, recv_sem, device):
        return pltpu.make_async_remote_copy(
            src_ref=src, dst_ref=dst, send_sem=send_sem, recv_sem=recv_sem,
            device_id=device, device_id_type=MESH)

    def x_copy(i):
        return remote(video.at[:, row_of(i, 1 - flip)], raw.at[pl.ds(mine, 2), i],
                      x_send.at[i], x_recv.at[i], partner)

    def x_wait(i):
        at = raw.at[pl.ds(theirs, 2), i]
        remote(at, at, x_send.at[i], x_recv.at[i], partner).wait_recv()

    def z_copy(i):
        return remote(video.at[:, row_of(i, flip)], raw.at[0:2, i], z_send.at[i], z_recv.at[i], below)

    def z_forward(i):
        return remote(raw.at[4:6, i], raw.at[0:2, i], z_send.at[i], z_recv.at[i], below)

    def z_wait(i):
        z_forward(i).wait_recv()

    def c_copy():
        return remote(raw.at[0:2, 2], raw.at[0:2, 3], c_send, z_recv.at[3], partner)

    def e_copy(j):
        src = (raw.at[0:2, 1], raw.at[2:4, 1], video.at[:, row_of(1, flip)])[j]
        return remote(src, raw.at[2 * j:2 * j + 2, 0], e_send.at[j], e_recv.at[j], other)

    x_copy(1).start()
    x_copy(2).start()

    @pl.when(odd)
    def _():
        e_copy(2).start()

    @pl.when(odd & has_down)
    def _():
        for i in (1, 2):
            z_copy(i).start()

    @pl.when(even)
    def _():
        for e in range(6):
            act[e, 0] = jnp.zeros((cols, 3 * chans), bf)

    @pl.when(jnp.logical_not(has_up))
    def _():
        for e in range(2):
            for i in range(4):
                act[e, i] = jnp.zeros((cols, 3 * chans), bf)
        for r in range(half):
            for s in range(own - 1, REACH):
                nb[r, s] = jnp.zeros((cols, chans), bf)

    @pl.when(jnp.logical_not(has_far))
    def _():
        for r in range(half):
            for s in range(own - 1):
                nb[r, s] = jnp.zeros((cols, chans), bf)

    head_of = [lax.broadcasted_iota(jnp.int32, (chans, chans), d) // HD for d in range(2)]
    gather[...] = jnp.where(head_of[0] == head_of[1], HD ** (-0.5), 0.0).astype(bf)

    col = lax.broadcasted_iota(jnp.int32, (cols, chans), 0)

    def activate(e, i):
        v = normalize(raw[e, i].astype(jnp.float32))
        v = v / (1.0 + jnp.exp(-v))
        act[e, i, :, chans:2 * chans] = v.astype(bf)
        left = jnp.where(col == 0, 0.0, pltpu.roll(v, 1, 0))
        right = jnp.where(col == cols - 1, 0.0, pltpu.roll(v, cols - 1, 0))
        act[e, i, :, 0:chans] = left.astype(bf)
        act[e, i, :, 2 * chans:3 * chans] = right.astype(bf)

    def activate_two(e, i):
        activate(e, i)
        activate(e + 1, i)

    def taps(e, line, size, a):
        total = None
        for o in range(3):
            window = act[pl.ds(e, 2), line + o - 1:line + o - 1 + size]
            term = jnp.dot(window.reshape(2 * size * cols, 3 * chans), cw[a, o + flip * (2 - 2 * o)],
                           preferred_element_type=jnp.float32)
            total = term if total is None else total + term
        return total

    for i in (1, 2, 3):
        loads[i].wait()
        activate_two(mine, i)

    @pl.when(odd)
    def _():
        e_copy(2).wait_recv()
        activate_two(4, 0)

    weight_load(first_tap).wait()
    acc[1] = taps(mine, 1, 2, first_tap).reshape(2, half, cols, chans)
    x_copy(3).start()

    @pl.when(odd & has_down)
    def _():
        z_copy(3).start()


    def nb_copy(m, r):
        src, dst = ((slice(REACH + 2, REACH + 4), slice(5, 7)),
                    (slice(REACH, REACH + 2), slice(3, 5)),
                    (slice(6, 7), slice(2, 3)),
                    (slice(5, 6), slice(1, 2)),
                    (slice(4, 5), slice(0, 1)))[m]
        return remote(nb.at[r, src], nb.at[r, dst], nb_send.at[m, r], nb_recv.at[m, r], below)

    def finish(pair, r, total):
        mixed = raw[2 + 2 * pair:4 + 2 * pair, 1 + r].astype(jnp.float32) + total.reshape(2, cols, chans)
        hidden = mixed.astype(bf)
        hid[r, 2 * pair:2 * pair + 2] = hidden
        nb[r, REACH + 2 * pair:REACH + 2 * pair + 2] = normalize(hidden.astype(jnp.float32)).astype(bf)

        @pl.when(has_down)
        def _():
            nb_copy(1 - pair, r).start()

    def late(r):
        total = acc[1, :, r].reshape(2 * cols, chans)
        total = total + taps(theirs, 1 + r, 1, last_tap) + taps(3, 1 + r, 1, 1)
        finish(1, r, total)

    def early(r):
        total = acc[0, :, r].reshape(2 * cols, chans)
        total = total + taps(1, 1 + r, 1, 1) + taps(0, 1 + r, 1, 0)
        finish(0, r, total)

    for i in (1, 2):
        x_wait(i)

        @pl.when(even & has_down)
        def _(i=i):
            z_forward(i).start()

        if i == 1:
            @pl.when(odd)
            def _():
                e_copy(1).start()
        activate_two(theirs, i)

    @pl.when(odd)
    def _():
        e_copy(1).wait_recv()
        activate_two(2, 0)

    @pl.when(odd & has_up)
    def _():
        z_wait(1)
        e_copy(0).start()

    weight_load(1).wait()
    weight_load(last_tap).wait()
    late(0)
    x_wait(3)

    @pl.when(odd & has_up)
    def _():
        z_wait(2)
        c_copy().start()

    activate_two(theirs, 3)
    late(1)

    acc[0] = taps(2, 1, 2, 2).reshape(2, half, cols, chans)

    @pl.when(odd & has_up)
    def _():
        activate_two(0, 1)
        activate_two(0, 2)
        e_copy(0).wait_recv()
        activate_two(0, 0)

    @pl.when(even & has_up)
    def _():
        z_wait(1)
        activate_two(0, 1)
        z_wait(2)
        activate_two(0, 2)

    early(0)

    @pl.when(has_up)
    def _():
        z_wait(3)
        activate_two(0, 3)

    early(1)

    for load in p_loads:
        load.wait()

    def keyed(r, start, size):
        x = nb[r, start:start + size].reshape(size * cols, chans)
        got = jnp.dot(x, pw[:, chans:3 * chans], preferred_element_type=jnp.float32).astype(bf)
        ks[r, start:start + size] = got[:, :chans].reshape(size, cols, chans)
        vs[r, start:start + size] = got[:, chans:].reshape(size, cols, chans)

    def asked(r):
        x = nb[r, REACH:REACH + own].reshape(own * cols, chans)
        got = jnp.dot(x, pw[:, :chans], preferred_element_type=jnp.float32).astype(bf)
        qs[r] = got.reshape(own, cols, chans)

    frames = ids.shape[0]
    first = 2 * (me - side)
    key_ids = [ids[lax.rem(first - REACH + s + frames, frames)] for s in range(REACH + own)]
    bias = {}
    for f in range(own):
        for s in range(f, f + REACH + 1):
            allowed = (first - REACH + s >= 0) & (key_ids[s] >= key_ids[REACH + f] - 1)
            bias[f, s] = jnp.where(allowed, 0.0, -1e30)

    def scored(r, pairs):
        prods = [qs[r, f] * ks[r, s] for f, s in pairs]
        got = jnp.dot(jnp.concatenate(prods, axis=0), gather[...], preferred_element_type=jnp.float32)
        return [got[at * cols:(at + 1) * cols] + bias[pair] for at, pair in enumerate(pairs)]

    def out_copy(r, f):
        at = out.at[f % 2, row_of(1 + r, flip)]
        keep = pltpu.make_async_copy(enc.at[r, f], at, own_out.at[r, f % 2])
        give = remote(enc.at[r, f], at, out_send.at[r, f % 2], out_recv.at[r, f % 2], partner)
        return keep, give

    def out_wait(r, f):
        at = out.at[f, row_of(1 + r, 1 - flip)]
        remote(enc.at[r, f], at, out_send.at[r, f], out_recv.at[r, f], partner).wait_recv()

    def settle(r, f, total, got):
        mixed = jnp.dot((got / total).astype(bf), pw[:, 3 * chans:], preferred_element_type=jnp.float32)
        enc[r, f] = (mixed + hid[r, f].astype(jnp.float32)).astype(bf)
        keep, give = out_copy(r, f)

        @pl.when(side == f // 2)
        def _():
            keep.start()

        @pl.when(side != f // 2)
        def _():
            give.start()

    def near(r, f):
        keys = range(own - 1, f + REACH + 1)
        scores = scored(r, [(f, s) for s in keys])
        top = functools.reduce(jnp.maximum, scores)
        total = got = None
        for s, score in zip(keys, scores):
            weight = jnp.exp(score - top)
            term = weight * vs[r, s].astype(jnp.float32)
            total = weight if total is None else total + weight
            got = term if got is None else got + term
        if f == own - 1:
            settle(r, f, total, got)
        else:
            tops[r, f], totals[r, f], gots[r, f] = top, total, got

    def far(r, s):
        queries = range(s, -1, -1)
        for f, score in zip(queries, scored(r, [(f, s) for f in queries])):
            top = jnp.maximum(tops[r, f], score)
            shrink = jnp.exp(tops[r, f] - top)
            weight = jnp.exp(score - top)
            total = totals[r, f] * shrink + weight
            got = gots[r, f] * shrink + weight * vs[r, s].astype(jnp.float32)
            if f == s:
                settle(r, f, total, got)
            else:
                tops[r, f], totals[r, f], gots[r, f] = top, total, got

    def take(m, r):
        @pl.when(has_up if m < 2 else has_far)
        def _():
            nb_copy(m, r).wait_recv()

    def relay(r, which_ones):
        @pl.when(inside)
        def _():
            for m in which_ones:
                nb_copy(m, r).start()

    for r in range(half):
        asked(r)
        keyed(r, REACH, own)
    take(0, 0)
    relay(0, (2, 3))
    keyed(0, 5, 2)
    take(1, 0)
    relay(0, (4,))
    take(0, 1)
    relay(1, (2, 3))
    keyed(0, 3, 2)
    keyed(1, 5, 2)
    for f in range(own - 1, -1, -1):
        near(0, f)
    take(1, 1)
    relay(1, (4,))
    keyed(1, 3, 2)
    for f in range(own - 1, -1, -1):
        near(1, f)
    for r in range(half):
        for s in range(own - 2, -1, -1):
            take(4 - s, r)
            keyed(r, s, 1)
            far(r, s)

    for i in (1, 2, 3):
        x_copy(i).wait_send()

    @pl.when(has_down)
    def _():
        z_forward(1).wait_send()
        z_forward(2).wait_send()
        for r in range(half):
            nb_copy(0, r).wait_send()
            nb_copy(1, r).wait_send()

    @pl.when(odd & has_down)
    def _():
        z_forward(3).wait_send()

    @pl.when(inside)
    def _():
        for r in range(half):
            for m in (2, 3, 4):
                nb_copy(m, r).wait_send()

    @pl.when(odd)
    def _():
        e_copy(1).wait_send()
        e_copy(2).wait_send()

    @pl.when(odd & has_up)
    def _():
        e_copy(0).wait_send()
        c_copy().wait_send()

    for r in range(half):
        for f in range(2):
            keep, give = out_copy(r, f)
            keep.wait()
            give.wait_send()
            out_wait(r, f)


def per_device(video, block_ids, conv_weight, w_query, w_key, w_value, w_output):
    count, rows, cols, chans = video.shape
    n = lax.axis_size("tm")
    assert count == 2 and n % 2 == 0 and n >= 4 and lax.axis_size("height") == 2
    assert rows == 4
    half = rows // 2
    own = 2 * count
    seen = REACH + own
    bf = jnp.bfloat16
    dma = pltpu.SemaphoreType.DMA
    anywhere = pl.BlockSpec(memory_space=pl.ANY)
    operands = [pltpu.with_memory_space_constraint(v, pltpu.HBM) for v in (
        block_ids, video, conv_weight.reshape(3, 3, 3 * chans, chans), w_query, w_key, w_value, w_output)]
    return pl.pallas_call(
        functools.partial(kernel, n),
        out_shape=jax.ShapeDtypeStruct(video.shape, bf),
        in_specs=[pl.BlockSpec(memory_space=pltpu.SMEM)] + [anywhere] * 6,
        out_specs=anywhere,
        scratch_shapes=[
            pltpu.VMEM((6, 4, cols, chans), bf),
            pltpu.VMEM((6, 4, cols, 3 * chans), bf),
            pltpu.VMEM((3, 3, 3 * chans, chans), bf),
            pltpu.VMEM((chans, 4 * chans), bf),
            pltpu.VMEM((2, 2, half, cols, chans), jnp.float32),
            pltpu.VMEM((half, own, cols, chans), bf),
            pltpu.VMEM((half, seen, cols, chans), bf),
            pltpu.VMEM((half, own, cols, chans), bf),
            pltpu.VMEM((half, seen, cols, chans), bf),
            pltpu.VMEM((half, seen, cols, chans), bf),
            pltpu.VMEM((half, own - 1, cols, chans), jnp.float32),
            pltpu.VMEM((half, own - 1, cols, chans), jnp.float32),
            pltpu.VMEM((half, own - 1, cols, chans), jnp.float32),
            pltpu.VMEM((half, own, cols, chans), bf),
            pltpu.VMEM((chans, chans), bf),
            dma((4,)),
            dma((7,)),
            dma((4,)),
            dma((4,)),
            dma((4,)),
            dma((4,)),
            dma,
            dma((3,)),
            dma((3,)),
            dma((5, half)),
            dma((5, half)),
            dma((half, 2)),
            dma((half, 2)),
            dma((half, 2)),
        ],
        compiler_params=pltpu.CompilerParams(
            collective_id=0, has_side_effects=True, vmem_limit_bytes=40 * 1024 * 1024),
    )(*operands)


def solution(mesh):
    placed = (P(("groups", "tm"), "height", None, None), P("groups"), P(), P(), P(), P(), P())
    return jax.shard_map(
        per_device,
        mesh=mesh,
        in_specs=placed,
        out_specs=P(("groups", "tm"), "height", None, None),
        check_vma=False,
    )
```
